32 devices in a mesh: sec: 4 (over x, core), row: 4 (over z), col: 2 (over y).
Axes of the slice: x: 2, y: 2, z: 4, core: 2. Of those that a mesh axis runs over, the one named last changes fastest.
Arguments:
- forcing: float32 [4, 8192, 128], P('sec', ('row', 'col')), may hold values from -6 to 6
- inverse_factor: bfloat16 [4, 2, 8192, 8192], P('sec', None, 'col', 'row'), as said below
- diag_inverse: float32 [4, 2, 8192], P('sec', None, 'col'), may hold values from -0.6 to 0.6
- coupling: float32 [4, 2, 8192], P('sec', None, ('row', 'col')), may hold values from -0.8 to 0.8
Outputs:
- section_fields: float32 [4, 8192, 128], P('sec', ('row', 'col'))
The draws below stay inside these ranges and needn't reach their ends.
Inputs may be any that keep to these rules, and one draw needn't show every extreme that they name: `inverse_factor`: each section's factor is lower triangular: entries above the diagonal are zero in both parts.
All inputs are finite; a program needn't handle non-finite values.
Results may differ from the reference program's by a relative error of at most 0.03.
Values may be sent and summed in bfloat16 or wider, within the bound.
A program may use at most 128 MiB of HBM per device.

```python
import jax
import jax.numpy as jnp
from jax import lax

F = 8192
R = 64
SECTIONS = 4
N_ROW = 4
N_COL = 2


def draw_inverse_factor(key, part):

    def one_section(index):
        section_key = jax.random.fold_in(key, index)
        values = jax.random.normal(section_key, (2, F, F), jnp.float32)
        rows = lax.broadcasted_iota(jnp.int32, (F, F), 0)
        cols = lax.broadcasted_iota(jnp.int32, (F, F), 1)
        lower = cols < rows
        diagonal = cols == rows
        reach = (rows - cols).astype(jnp.float32) / F
        spread = (0.3 + 2.4 * reach) / F ** 0.5
        real_part = jnp.where(lower, values[0] * spread, jnp.where(diagonal, 1.0, 0.0))
        imag_part = jnp.where(lower, values[1] * spread, jnp.where(diagonal, 0.5 * jnp.sin(values[1] * 3.0), 0.0))
        return jnp.stack([real_part, imag_part], axis=0).astype(jnp.bfloat16)
    return lax.map(one_section, jnp.arange(SECTIONS, dtype=jnp.int32))


def draw_forcing(key, part):
    value_key = jax.random.fold_in(key, 11)
    values = jnp.clip(jax.random.normal(value_key, (SECTIONS, F, 2 * R), jnp.float32), -6.0, 6.0)
    section = lax.broadcasted_iota(jnp.int32, (SECTIONS, 1, 1), 0)
    scale = jnp.where(section == 0, 1.0, 0.08)
    return (values * scale).astype(jnp.float32)


def draw_coupling(key, part):
    sign_key = jax.random.fold_in(key, 21)
    size_key = jax.random.fold_in(key, 22)
    signs = jnp.where(jax.random.uniform(sign_key, (SECTIONS, 2, F), jnp.float32) < 0.5, 1.0, -1.0)
    sizes = jax.random.uniform(size_key, (SECTIONS, 2, F), jnp.float32, 0.4, 0.8)
    return (signs * sizes).astype(jnp.float32)


def level_of(stream_key, dims, pieces, smallest, high):
    gain, own = 1.0, jax.random.fold_in(stream_key, 6)
    for position, parts in pieces:
        draws = jnp.exp(jax.random.uniform(jax.random.fold_in(own, position), (parts,), jnp.float32, smallest / len(pieces), high / len(pieces)))
        gain = gain * jnp.repeat(draws, dims[position] // parts).reshape([-1 if axis == position else 1 for axis in range(len(dims))])
    return gain


def setup_inputs(seed: int = 0) -> dict:
    arg_keys = jax.random.split(jax.random.key(seed), 5)
    forcing = draw_forcing(jax.random.fold_in(arg_keys[4], 71), 0)
    inverse_factor = draw_inverse_factor(jax.random.fold_in(arg_keys[4], 71), 0)
    diag_inverse = jnp.clip(jax.random.uniform(arg_keys[2], (SECTIONS, 2, F), jnp.float32, -0.6, 0.6) * level_of(arg_keys[2], (SECTIONS, 2, F), ((0, 4), (2, 2)), -0.4, 0.0), -0.6, 0.6)
    coupling = draw_coupling(jax.random.fold_in(arg_keys[4], 71), 0)
    return dict(forcing=forcing, inverse_factor=inverse_factor, diag_inverse=diag_inverse, coupling=coupling)


def complex_rows(coef_re, coef_im, values, half):
    v_re = values[:, :half]
    v_im = values[:, half:]
    out_re = coef_re[:, None] * v_re - coef_im[:, None] * v_im
    out_im = coef_re[:, None] * v_im + coef_im[:, None] * v_re
    return jnp.concatenate([out_re, out_im], axis=1)


def combine_parts(prod_re, prod_im, half):
    out_re = prod_re[:, :half] - prod_im[:, half:]
    out_im = prod_re[:, half:] + prod_im[:, :half]
    return jnp.concatenate([out_re, out_im], axis=1)


def forward_product(factor, source, half):
    width = factor.shape[2] // N_ROW
    total = jnp.zeros((factor.shape[1], source.shape[1]), jnp.float32)
    for block in range(N_ROW):
        lo = block * width
        piece = source[lo:lo + width]
        part_re = jnp.dot(factor[0][:, lo:lo + width], piece, preferred_element_type=jnp.float32)
        part_im = jnp.dot(factor[1][:, lo:lo + width], piece, preferred_element_type=jnp.float32)
        partial_sum = combine_parts(part_re, part_im, half).astype(jnp.bfloat16).astype(jnp.float32)
        total = total + partial_sum
    return total


def back_product(factor, scaled, half):
    width = factor.shape[1] // N_COL
    total = jnp.zeros((factor.shape[2], scaled.shape[1]), jnp.float32)
    for block in range(N_COL):
        lo = block * width
        piece = scaled[lo:lo + width]
        part_re = jnp.dot(factor[0][lo:lo + width].T, piece, preferred_element_type=jnp.float32)
        part_im = jnp.dot(factor[1][lo:lo + width].T, piece, preferred_element_type=jnp.float32)
        partial_sum = combine_parts(part_re, part_im, half).astype(jnp.bfloat16).astype(jnp.float32)
        total = total + partial_sum
    return total


def reference(forcing, inverse_factor, diag_inverse, coupling):
    half = forcing.shape[2] // 2
    previous = jnp.zeros(forcing.shape[1:], jnp.float32)
    results = []
    for section in range(SECTIONS):
        factor = inverse_factor[section]
        couple = coupling[section]
        source = (forcing[section] - complex_rows(couple[0], couple[1], previous, half)).astype(jnp.bfloat16)
        forward = forward_product(factor, source, half)
        dinv = diag_inverse[section]
        scaled = complex_rows(dinv[0], dinv[1], forward, half).astype(jnp.bfloat16)
        field = back_product(factor, scaled, half)
        results.append(field)
        previous = field
    return jnp.stack(results, axis=0)
```

```python
import functools

import jax
import jax.numpy as jnp
from jax import lax
from jax.experimental import pallas as pl
from jax.experimental.pallas import tpu as pltpu
from jax.sharding import PartitionSpec as P


def shifted(value, axis, steps):
    count = lax.axis_size(axis)
    initial, last = (max(0, -steps), min(count, count - steps))
    return lax.ppermute(value, axis, [(source, source + steps) for source in range(initial, last)])


def complex_rows(coef_re, coef_im, values, half):
    v_re = values[:, :half]
    v_im = values[:, half:]
    out_re = coef_re[:, None] * v_re - coef_im[:, None] * v_im
    out_im = coef_re[:, None] * v_im + coef_im[:, None] * v_re
    return jnp.concatenate([out_re, out_im], axis=1)


def combine_stack(product):
    half = product.shape[2] // 2
    out_re = product[0, :, :half] - product[1, :, half:]
    out_im = product[0, :, half:] + product[1, :, :half]
    return jnp.concatenate([out_re, out_im], axis=1)


def solve_section(source, factor, dinv):
    width = source.shape[1]
    product = jnp.einsum(
        "kij,jb->kib",
        factor,
        lax.all_gather(source, "col", axis=0, tiled=True),
        preferred_element_type=jnp.float32,
    )
    forward = combine_stack(product)
    share = lax.psum_scatter(
        forward.astype(jnp.bfloat16), "row", scatter_dimension=0, tiled=True
    ).astype(jnp.float32)
    share_rows = share.shape[0]
    local_dinv = lax.dynamic_slice_in_dim(dinv, lax.axis_index("row") * share_rows, share_rows, 1)
    scaled = complex_rows(local_dinv[0], local_dinv[1], share, width // 2).astype(jnp.bfloat16)
    product = jnp.einsum(
        "kij,ib->kjb",
        factor,
        lax.all_gather(scaled, "row", axis=0, tiled=True),
        preferred_element_type=jnp.float32,
    )
    back = combine_stack(product)
    return lax.psum_scatter(
        back.astype(jnp.bfloat16), "col", scatter_dimension=0, tiled=True
    ).astype(jnp.float32)


def local(forcing, inverse_factor, diag_inverse, coupling):
    sections = lax.axis_size("sec")
    section_id = lax.axis_index("sec")
    local_rhs = forcing[0]
    factor = inverse_factor[0]
    dinv = diag_inverse[0]
    couple = coupling[0]
    rows_here = local_rhs.shape[0]
    half = local_rhs.shape[1] // 2
    block_count = 1
    block_width = half // block_count
    rhs_blocks = local_rhs.reshape(rows_here, 2, block_count, block_width)
    results = jnp.zeros((rows_here, 2, block_count, block_width), jnp.float32)
    outgoing = jnp.zeros((rows_here, 2 * block_width), jnp.float32)
    for step_index in range(block_count + sections - 1):
        if step_index > 0:
            incoming = shifted(outgoing.astype(jnp.bfloat16), "sec", 1).astype(outgoing.dtype)
        else:
            incoming = jnp.zeros((rows_here, 2 * block_width), jnp.float32)
        block_index = step_index - section_id
        active = jnp.logical_and(block_index >= 0, block_index < block_count)
        safe_index = jnp.clip(block_index, 0, block_count - 1)
        current = lax.dynamic_index_in_dim(rhs_blocks, safe_index, 2, keepdims=False)
        current = current.reshape(rows_here, 2 * block_width)
        source = (current - complex_rows(couple[0], couple[1], incoming, block_width)).astype(
            jnp.bfloat16
        )
        field = solve_section(source, factor, dinv)
        updated = lax.dynamic_update_index_in_dim(
            results, field.reshape(rows_here, 2, block_width), safe_index, 2
        )
        results = jnp.where(active, updated, results)
        outgoing = field
    return results.reshape(1, rows_here, 2 * half)


MESH = pl.DeviceIdType.MESH


def sweep_kernel(
    n_sec, n_row, n_col, forcing, dinv, coupling, factor_hbm, out,
    factor, src_a, src_b, part_out, part_in, own, scaled, back,
    cross_out, cross_in, prev_out, prev_in, forcing_t,
    load_sem, src_send, src_recv, part_send, part_recv,
    sc_send, sc_recv, cross_send, cross_recv, prev_send, prev_recv,
):
    share = own.shape[0]
    half = own.shape[1] // 2
    block_rows = n_row * share
    block_cols = n_col * share
    s, r, c = lax.axis_index("sec"), lax.axis_index("row"), lax.axis_index("col")

    def meets(row, piece, col):
        return row * block_cols < col * block_rows + (piece + 1) * share

    def piece_rows(piece):
        return pl.ds(pl.multiple_of(piece * share, share), share)

    def load(k):
        rows = piece_rows(lax.rem(r + k, n_row))
        return pltpu.make_async_copy(
            factor_hbm.at[0, :, rows, :], factor.at[:, rows, :], load_sem.at[k]
        )

    def send_source(j):
        return pltpu.make_async_remote_copy(
            src_ref=src_a.at[piece_rows(c)], dst_ref=src_a.at[piece_rows(c)],
            send_sem=src_send.at[j - 1], recv_sem=src_recv.at[j - 1],
            device_id=(s, r, lax.rem(c + j, n_col)), device_id_type=MESH,
        )

    def send_part(k):
        return pltpu.make_async_remote_copy(
            src_ref=part_out.at[k - 1], dst_ref=part_in.at[k - 1],
            send_sem=part_send.at[k - 1], recv_sem=part_recv.at[k - 1],
            device_id=(s, lax.rem(r + k, n_row), c), device_id_type=MESH,
        )

    def send_scaled(k):
        return pltpu.make_async_remote_copy(
            src_ref=scaled.at[r], dst_ref=scaled.at[r],
            send_sem=sc_send.at[k - 1], recv_sem=sc_recv.at[k - 1],
            device_id=(s, lax.rem(r + k, n_row), c), device_id_type=MESH,
        )

    def send_cross(j):
        return pltpu.make_async_remote_copy(
            src_ref=cross_out.at[j - 1], dst_ref=cross_in.at[j - 1],
            send_sem=cross_send.at[j - 1], recv_sem=cross_recv.at[j - 1],
            device_id=(s, r, lax.rem(c + j, n_col)), device_id_type=MESH,
        )

    def send_prev():
        return pltpu.make_async_remote_copy(
            src_ref=prev_out, dst_ref=prev_in, send_sem=prev_send, recv_sem=prev_recv,
            device_id=(lax.rem(s + 1, n_sec), r, c), device_id_type=MESH,
        )

    order = list(range(1, n_row)) + [0]
    for k in order:
        @pl.when(meets(r, lax.rem(r + k, n_row), c))
        def _(k=k):
            load(k).start()

    barrier = pltpu.get_barrier_semaphore()
    for k in range(1, n_row):
        pl.semaphore_signal(barrier, 1, device_id=(s, lax.rem(r + k, n_row), c), device_id_type=MESH)
    for j in range(1, n_col):
        pl.semaphore_signal(barrier, 1, device_id=(s, r, lax.rem(c + j, n_col)), device_id_type=MESH)
    for step in (1, n_sec - 1):
        pl.semaphore_signal(barrier, 1, device_id=(lax.rem(s + step, n_sec), r, c), device_id_type=MESH)
    pl.semaphore_wait(barrier, n_row + n_col)

    def turned(value):
        return jnp.concatenate([-value[:, half:], value[:, :half]], axis=1)

    @pl.when(s == 0)
    def _():
        src_a[piece_rows(c), :] = forcing[0].astype(jnp.bfloat16)

    @pl.when(s > 0)
    def _():
        forcing_t[...] = forcing[0].T
        send_prev().wait_recv()
        previous = prev_in[...].astype(jnp.float32)
        p_re, p_im = previous[:half], previous[half:]
        c_re, c_im = coupling[0, 0:1, :], coupling[0, 1:2, :]
        new_re = forcing_t[:half] - (c_re * p_re - c_im * p_im)
        new_im = forcing_t[half:] - (c_re * p_im + c_im * p_re)
        new = jnp.concatenate([new_re, new_im], axis=0).T
        src_a[piece_rows(c), :] = new.astype(jnp.bfloat16)

    for j in range(1, n_col):
        send_source(j).start()
    for j in range(n_col):
        if j > 0:
            send_source(j).wait_recv()
        rows = piece_rows(lax.rem(c - j + n_col, n_col))
        src_b[rows, :] = turned(src_a[rows, :].astype(jnp.float32)).astype(jnp.bfloat16)

    tile = min(512, share)
    for k in order:
        piece = lax.rem(r + k, n_row)
        wanted = meets(r, piece, c)

        @pl.when(wanted)
        def _(k=k, piece=piece):
            load(k).wait()

            @pl.loop(0, share // tile)
            def _(t):
                rows = pl.ds(pl.multiple_of(piece * share + t * tile, tile), tile)
                here = pl.ds(pl.multiple_of(t * tile, tile), tile)
                total = jnp.dot(factor[0, rows, :], src_a[...], preferred_element_type=jnp.float32)
                total += jnp.dot(factor[1, rows, :], src_b[...], preferred_element_type=jnp.float32)
                if k == 0:
                    own[here, :] = total
                else:
                    part_out[k - 1, here, :] = total.astype(jnp.bfloat16)

            if k > 0:
                send_part(k).start()

        if k == 0:
            @pl.when(jnp.logical_not(wanted))
            def _():
                own[...] = jnp.zeros_like(own)

    for k in range(1, n_row):
        @pl.when(meets(lax.rem(r - k + n_row, n_row), r, c))
        def _(k=k):
            send_part(k).wait_recv()
            own[...] += part_in[k - 1].astype(jnp.float32)

    forward = own[...].T
    d_re, d_im = dinv[0, 0:1, piece_rows(r)], dinv[0, 1:2, piece_rows(r)]
    f_re, f_im = forward[:half], forward[half:]
    scaled[r] = jnp.concatenate(
        [d_re * f_re - d_im * f_im, d_re * f_im + d_im * f_re], axis=0
    ).astype(jnp.bfloat16)
    for k in range(1, n_row):
        @pl.when(meets(lax.rem(r + k, n_row), r, c))
        def _(k=k):
            send_scaled(k).start()

    back[...] = jnp.zeros_like(back)
    width = min(512, block_cols)
    for k in range(n_row):
        piece = lax.rem(r - k + n_row, n_row)

        @pl.when(meets(r, piece, c))
        def _(k=k, piece=piece):
            if k > 0:
                send_scaled(k).wait_recv()
            rows = piece_rows(piece)
            lhs = scaled[piece]
            lhs_b = jnp.concatenate([-lhs[half:], lhs[:half]], axis=0)

            @pl.loop(0, block_cols // width)
            def _(t):
                cols = pl.ds(pl.multiple_of(t * width, width), width)
                total = jnp.dot(lhs, factor[0, rows, cols], preferred_element_type=jnp.float32)
                total += jnp.dot(lhs_b, factor[1, rows, cols], preferred_element_type=jnp.float32)
                back[:, cols] += total

    filled = meets(r, n_row - 1, c)
    for j in range(1, n_col):
        @pl.when(filled)
        def _(j=j):
            cross_out[j - 1] = back[:, piece_rows(lax.rem(c + j, n_col))].astype(jnp.bfloat16)
            send_cross(j).start()

    forcing_t[...] = back[:, piece_rows(c)]
    for j in range(1, n_col):
        @pl.when(meets(r, n_row - 1, lax.rem(c - j + n_col, n_col)))
        def _(j=j):
            send_cross(j).wait_recv()
            forcing_t[...] += cross_in[j - 1].astype(jnp.float32)

    @pl.when(s < n_sec - 1)
    def _():
        prev_out[...] = forcing_t[...].astype(jnp.bfloat16)
        send_prev().start()

    out[0] = forcing_t[...].T

    for j in range(1, n_col):
        send_source(j).wait_send()

        @pl.when(filled)
        def _(j=j):
            send_cross(j).wait_send()

    for k in range(1, n_row):
        @pl.when(meets(r, lax.rem(r + k, n_row), c))
        def _(k=k):
            send_part(k).wait_send()

        @pl.when(meets(lax.rem(r + k, n_row), r, c))
        def _(k=k):
            send_scaled(k).wait_send()

    @pl.when(s < n_sec - 1)
    def _():
        send_prev().wait_send()


def sweep(n_sec, n_row, n_col, forcing, inverse_factor, diag_inverse, coupling):
    share, width = forcing.shape[1:]
    block_rows, block_cols = inverse_factor.shape[2:]
    vmem = pl.BlockSpec(memory_space=pltpu.VMEM)
    bf16, f32 = jnp.bfloat16, jnp.float32
    dma = pltpu.SemaphoreType.DMA
    rows_out, cols_out = max(n_row - 1, 1), max(n_col - 1, 1)
    return pl.pallas_call(
        functools.partial(sweep_kernel, n_sec, n_row, n_col),
        out_shape=jax.ShapeDtypeStruct(forcing.shape, f32),
        in_specs=[vmem, vmem, vmem, pl.BlockSpec(memory_space=pl.ANY)],
        out_specs=vmem,
        scratch_shapes=[
            pltpu.VMEM((2, block_rows, block_cols), bf16),
            pltpu.VMEM((block_cols, width), bf16),
            pltpu.VMEM((block_cols, width), bf16),
            pltpu.VMEM((rows_out, share, width), bf16),
            pltpu.VMEM((rows_out, share, width), bf16),
            pltpu.VMEM((share, width), f32),
            pltpu.VMEM((n_row, width, share), bf16),
            pltpu.VMEM((width, block_cols), f32),
            pltpu.VMEM((cols_out, width, share), bf16),
            pltpu.VMEM((cols_out, width, share), bf16),
            pltpu.VMEM((width, share), bf16),
            pltpu.VMEM((width, share), bf16),
            pltpu.VMEM((width, share), f32),
            dma((n_row,)),
            dma((cols_out,)), dma((cols_out,)),
            dma((rows_out,)), dma((rows_out,)),
            dma((rows_out,)), dma((rows_out,)),
            dma((cols_out,)), dma((cols_out,)),
            dma, dma,
        ],
        compiler_params=pltpu.CompilerParams(
            collective_id=0, has_side_effects=True, vmem_limit_bytes=56 * 2**20
        ),
    )(forcing, diag_inverse, coupling, inverse_factor)


def solution(mesh):
    placed = (
        P("sec", ("row", "col"), None),
        P("sec", None, "col", "row"),
        P("sec", None, "col"),
        P("sec", None, ("row", "col")),
    )
    n_sec, n_row, n_col = (mesh.shape[axis] for axis in ("sec", "row", "col"))

    def body(forcing, inverse_factor, diag_inverse, coupling):
        share, width = forcing.shape[1:]
        fits = inverse_factor.size * 2 <= 32 * 2**20
        if share % 128 or width % 128 or not fits or n_sec < 3:
            return local(forcing, inverse_factor, diag_inverse, coupling)
        return sweep(n_sec, n_row, n_col, forcing, inverse_factor, diag_inverse, coupling)

    return jax.shard_map(
        body, mesh=mesh, in_specs=placed, out_specs=P("sec", ("row", "col"), None), check_vma=False
    )
```

```python
import functools

import jax
import jax.numpy as jnp
from jax import lax
from jax.experimental import pallas as pl
from jax.experimental.pallas import tpu as pltpu
from jax.sharding import PartitionSpec as P


def shifted(value, axis, steps):
    count = lax.axis_size(axis)
    initial, last = (max(0, -steps), min(count, count - steps))
    return lax.ppermute(value, axis, [(source, source + steps) for source in range(initial, last)])


def complex_rows(coef_re, coef_im, values, half):
    v_re = values[:, :half]
    v_im = values[:, half:]
    out_re = coef_re[:, None] * v_re - coef_im[:, None] * v_im
    out_im = coef_re[:, None] * v_im + coef_im[:, None] * v_re
    return jnp.concatenate([out_re, out_im], axis=1)


def combine_stack(product):
    half = product.shape[2] // 2
    out_re = product[0, :, :half] - product[1, :, half:]
    out_im = product[0, :, half:] + product[1, :, :half]
    return jnp.concatenate([out_re, out_im], axis=1)


def solve_section(source, factor, dinv):
    width = source.shape[1]
    product = jnp.einsum(
        "kij,jb->kib",
        factor,
        lax.all_gather(source, "col", axis=0, tiled=True),
        preferred_element_type=jnp.float32,
    )
    forward = combine_stack(product)
    share = lax.psum_scatter(
        forward.astype(jnp.bfloat16), "row", scatter_dimension=0, tiled=True
    ).astype(jnp.float32)
    share_rows = share.shape[0]
    local_dinv = lax.dynamic_slice_in_dim(dinv, lax.axis_index("row") * share_rows, share_rows, 1)
    scaled = complex_rows(local_dinv[0], local_dinv[1], share, width // 2).astype(jnp.bfloat16)
    product = jnp.einsum(
        "kij,ib->kjb",
        factor,
        lax.all_gather(scaled, "row", axis=0, tiled=True),
        preferred_element_type=jnp.float32,
    )
    back = combine_stack(product)
    return lax.psum_scatter(
        back.astype(jnp.bfloat16), "col", scatter_dimension=0, tiled=True
    ).astype(jnp.float32)


def local(forcing, inverse_factor, diag_inverse, coupling):
    sections = lax.axis_size("sec")
    section_id = lax.axis_index("sec")
    local_rhs = forcing[0]
    factor = inverse_factor[0]
    dinv = diag_inverse[0]
    couple = coupling[0]
    rows_here = local_rhs.shape[0]
    half = local_rhs.shape[1] // 2
    block_count = 1
    block_width = half // block_count
    rhs_blocks = local_rhs.reshape(rows_here, 2, block_count, block_width)
    results = jnp.zeros((rows_here, 2, block_count, block_width), jnp.float32)
    outgoing = jnp.zeros((rows_here, 2 * block_width), jnp.float32)
    for step_index in range(block_count + sections - 1):
        if step_index > 0:
            incoming = shifted(outgoing.astype(jnp.bfloat16), "sec", 1).astype(outgoing.dtype)
        else:
            incoming = jnp.zeros((rows_here, 2 * block_width), jnp.float32)
        block_index = step_index - section_id
        active = jnp.logical_and(block_index >= 0, block_index < block_count)
        safe_index = jnp.clip(block_index, 0, block_count - 1)
        current = lax.dynamic_index_in_dim(rhs_blocks, safe_index, 2, keepdims=False)
        current = current.reshape(rows_here, 2 * block_width)
        source = (current - complex_rows(couple[0], couple[1], incoming, block_width)).astype(
            jnp.bfloat16
        )
        field = solve_section(source, factor, dinv)
        updated = lax.dynamic_update_index_in_dim(
            results, field.reshape(rows_here, 2, block_width), safe_index, 2
        )
        results = jnp.where(active, updated, results)
        outgoing = field
    return results.reshape(1, rows_here, 2 * half)


MESH = pl.DeviceIdType.MESH


def sweep_kernel(
    n_sec, n_row, n_col, forcing, dinv, coupling, factor_hbm, out,
    factor, src_a, src_b, part_out, part_in, own, scaled, back,
    cross_out, cross_in, prev_out, prev_in, forcing_t,
    coupling_all, result,
    load_sem, src_send, src_recv, part_send, part_recv,
    sc_send, sc_recv, cross_send, cross_recv, prev_send, prev_recv,
    rhs_send, rhs_recv, coef_send, coef_recv,
):
    share = own.shape[1]
    half = own.shape[2] // 2
    block_rows = n_row * share
    block_cols = n_col * share
    s, r, c = lax.axis_index("sec"), lax.axis_index("row"), lax.axis_index("col")

    def last_row(piece, col):
        return jnp.minimum(n_row - 1, (col * block_rows + (piece + 1) * share - 1) // block_cols)

    def piece_rows(piece):
        return pl.ds(pl.multiple_of(piece * share, share), share)

    def load(q):
        rows = piece_rows(q)
        return pltpu.make_async_copy(
            factor_hbm.at[0, :, rows, :], factor.at[:, rows, :], load_sem.at[q]
        )

    last = [last_row(q, c) for q in range(n_row)]
    owner = [(m + 1) // 2 for m in last]

    def send_source(j):
        return pltpu.make_async_remote_copy(
            src_ref=src_a.at[piece_rows(c)], dst_ref=src_a.at[piece_rows(c)],
            send_sem=src_send.at[j - 1], recv_sem=src_recv.at[j - 1],
            device_id=(s, r, lax.rem(c + j, n_col)), device_id_type=MESH,
        )

    def send_part(q, sender):
        return pltpu.make_async_remote_copy(
            src_ref=part_out.at[q], dst_ref=part_in.at[q, sender],
            send_sem=part_send.at[q], recv_sem=part_recv.at[q, sender],
            device_id=(s, owner[q], c), device_id_type=MESH,
        )

    def send_scaled(q, to):
        return pltpu.make_async_remote_copy(
            src_ref=scaled.at[q], dst_ref=scaled.at[q],
            send_sem=sc_send.at[q, to], recv_sem=sc_recv.at[q],
            device_id=(s, to, c), device_id_type=MESH,
        )

    def send_rhs(j):
        return pltpu.make_async_remote_copy(
            src_ref=forcing_t.at[c], dst_ref=forcing_t.at[c],
            send_sem=rhs_send.at[j - 1], recv_sem=rhs_recv.at[j - 1],
            device_id=(s, r, lax.rem(c + j, n_col)), device_id_type=MESH,
        )

    def send_coef(j):
        return pltpu.make_async_remote_copy(
            src_ref=coupling_all.at[c], dst_ref=coupling_all.at[c],
            send_sem=coef_send.at[j - 1], recv_sem=coef_recv.at[j - 1],
            device_id=(s, r, lax.rem(c + j, n_col)), device_id_type=MESH,
        )

    def send_cross(j):
        return pltpu.make_async_remote_copy(
            src_ref=cross_out.at[j - 1], dst_ref=cross_in.at[j - 1],
            send_sem=cross_send.at[j - 1], recv_sem=cross_recv.at[j - 1],
            device_id=(s, r, lax.rem(c + j, n_col)), device_id_type=MESH,
        )

    def send_prev(j):
        return pltpu.make_async_remote_copy(
            src_ref=prev_out, dst_ref=prev_in.at[j],
            send_sem=prev_send.at[j], recv_sem=prev_recv.at[j],
            device_id=(lax.rem(s + 1, n_sec), r, lax.rem(c + j, n_col)), device_id_type=MESH,
        )

    order = list(range(n_row - 1, -1, -1))
    for q in order:
        @pl.when(r <= last[q])
        def _(q=q):
            load(q).start()

    barrier = pltpu.get_barrier_semaphore()
    for i in range(1, n_row):
        pl.semaphore_signal(barrier, 1, device_id=(s, lax.rem(r + i, n_row), c), device_id_type=MESH)
    for j in range(1, n_col):
        pl.semaphore_signal(barrier, 1, device_id=(s, r, lax.rem(c + j, n_col)), device_id_type=MESH)
    for step in (1, n_sec - 1):
        for j in range(n_col):
            pl.semaphore_signal(
                barrier, 1, device_id=(lax.rem(s + step, n_sec), r, lax.rem(c + j, n_col)),
                device_id_type=MESH,
            )
    pl.semaphore_wait(barrier, n_row - 1 + n_col - 1 + 2 * n_col)

    def turned(value):
        return jnp.concatenate([-value[:, half:], value[:, :half]], axis=1)

    @pl.when(s == 0)
    def _():
        src_a[piece_rows(c), :] = forcing[0].astype(jnp.bfloat16)
        for j in range(1, n_col):
            send_source(j).start()
        for j in range(n_col):
            if j > 0:
                send_source(j).wait_recv()
            rows = piece_rows(lax.rem(c - j + n_col, n_col))
            src_b[rows, :] = turned(src_a[rows, :].astype(jnp.float32)).astype(jnp.bfloat16)

    @pl.when(s > 0)
    def _():
        forcing_t[c] = forcing[0].T
        coupling_all[c] = coupling[0]
        for j in range(1, n_col):
            send_rhs(j).start()
            send_coef(j).start()
        for j in range(1, n_col):
            send_rhs(j).wait_recv()
            send_coef(j).wait_recv()
        for j in range(n_col):
            col = lax.rem(c - j + n_col, n_col)
            rows = piece_rows(col)
            send_prev(j).wait_recv()
            previous = prev_in[j].astype(jnp.float32)
            p_re, p_im = previous[:half], previous[half:]
            c_re, c_im = coupling_all[col, 0:1, :], coupling_all[col, 1:2, :]
            new_re = forcing_t[col, :half] - (c_re * p_re - c_im * p_im)
            new_im = forcing_t[col, half:] - (c_re * p_im + c_im * p_re)
            src_a[rows, :] = jnp.concatenate([new_re, new_im], axis=0).T.astype(jnp.bfloat16)
            src_b[rows, :] = jnp.concatenate([-new_im, new_re], axis=0).T.astype(jnp.bfloat16)

    tile = min(512, share)

    def forward_piece(q):
        @pl.when(r <= last[q])
        def _():
            load(q).wait()
            mine = r == owner[q]

            @pl.loop(0, share // tile)
            def _(t):
                rows = pl.ds(pl.multiple_of(q * share + t * tile, tile), tile)
                here = pl.ds(pl.multiple_of(t * tile, tile), tile)
                total = jnp.dot(factor[0, rows, :], src_a[...], preferred_element_type=jnp.float32)
                total += jnp.dot(factor[1, rows, :], src_b[...], preferred_element_type=jnp.float32)
                own[q, here, :] = total
                part_out[q, here, :] = total.astype(jnp.bfloat16)

            @pl.when(jnp.logical_not(mine))
            def _():
                send_part(q, r).start()

    def reduce_piece(q):
        @pl.when(r == owner[q])
        def _():
            for p in range(n_row):
                @pl.when(jnp.logical_and(p != r, p <= last[q]))
                def _(p=p):
                    send_part(q, p).wait_recv()
                    own[q] += part_in[q, p].astype(jnp.float32)

            forward = own[q].T
            d_re, d_im = dinv[0, 0:1, pl.ds(q * share, share)], dinv[0, 1:2, pl.ds(q * share, share)]
            f_re, f_im = forward[:half], forward[half:]
            scaled[q] = jnp.concatenate(
                [d_re * f_re - d_im * f_im, d_re * f_im + d_im * f_re], axis=0
            ).astype(jnp.bfloat16)
            for p in range(n_row):
                @pl.when(jnp.logical_and(p != r, p <= last[q]))
                def _(p=p):
                    send_scaled(q, p).start()

    for i, q in enumerate(order):
        forward_piece(q)
        if i >= 2:
            reduce_piece(order[i - 2])
    for q in order[max(n_row - 2, 0):]:
        reduce_piece(q)

    back[...] = jnp.zeros_like(back)
    width = min(512, share)
    filled = r <= last[n_row - 1]
    turns = list(range(1, n_row, 2)) + list(range(0, n_row, 2))
    for q in turns:
        @pl.when(jnp.logical_and(r <= last[q], r != owner[q]))
        def _(q=q):
            send_scaled(q, r).wait_recv()

        for j in list(range(1, n_col)) + [0]:
            @pl.when(r <= last[q])
            def _(q=q, j=j):
                rows = piece_rows(q)
                lhs = scaled[q]
                lhs_b = jnp.concatenate([-lhs[half:], lhs[:half]], axis=0)

                @pl.loop(0, share // width)
                def _(t):
                    first = lax.rem(c + j, n_col) * share + t * width
                    cols = pl.ds(pl.multiple_of(first, width), width)
                    total = jnp.dot(lhs, factor[0, rows, cols], preferred_element_type=jnp.float32)
                    total += jnp.dot(lhs_b, factor[1, rows, cols], preferred_element_type=jnp.float32)
                    back[:, cols] += total

            if q == turns[-1] and j > 0:
                @pl.when(filled)
                def _(j=j):
                    cross_out[j - 1] = back[:, piece_rows(lax.rem(c + j, n_col))].astype(jnp.bfloat16)
                    send_cross(j).start()

    result[...] = back[:, piece_rows(c)]
    for j in range(1, n_col):
        @pl.when(r <= last_row(n_row - 1, lax.rem(c - j + n_col, n_col)))
        def _(j=j):
            send_cross(j).wait_recv()
            result[...] += cross_in[j - 1].astype(jnp.float32)

    @pl.when(s < n_sec - 1)
    def _():
        prev_out[...] = result[...].astype(jnp.bfloat16)
        for j in list(range(1, n_col)) + [0]:
            send_prev(j).start()

    out[0] = result[...].T

    @pl.when(s == 0)
    def _():
        for j in range(1, n_col):
            send_source(j).wait_send()

    @pl.when(s > 0)
    def _():
        for j in range(1, n_col):
            send_rhs(j).wait_send()
            send_coef(j).wait_send()

    @pl.when(filled)
    def _():
        for j in range(1, n_col):
            send_cross(j).wait_send()

    for q in range(n_row):
        @pl.when(jnp.logical_and(r <= last[q], r != owner[q]))
        def _(q=q):
            send_part(q, r).wait_send()

        for p in range(n_row):
            @pl.when(jnp.logical_and(r == owner[q], jnp.logical_and(p != r, p <= last[q])))
            def _(q=q, p=p):
                send_scaled(q, p).wait_send()

    @pl.when(s < n_sec - 1)
    def _():
        for j in range(n_col):
            send_prev(j).wait_send()


def sweep(n_sec, n_row, n_col, forcing, inverse_factor, diag_inverse, coupling):
    share, width = forcing.shape[1:]
    block_rows, block_cols = inverse_factor.shape[2:]
    vmem = pl.BlockSpec(memory_space=pltpu.VMEM)
    bf16, f32 = jnp.bfloat16, jnp.float32
    dma = pltpu.SemaphoreType.DMA
    cols_out = max(n_col - 1, 1)
    return pl.pallas_call(
        functools.partial(sweep_kernel, n_sec, n_row, n_col),
        out_shape=jax.ShapeDtypeStruct(forcing.shape, f32),
        in_specs=[vmem, vmem, vmem, pl.BlockSpec(memory_space=pl.ANY)],
        out_specs=vmem,
        scratch_shapes=[
            pltpu.VMEM((2, block_rows, block_cols), bf16),
            pltpu.VMEM((block_cols, width), bf16),
            pltpu.VMEM((block_cols, width), bf16),
            pltpu.VMEM((n_row, share, width), bf16),
            pltpu.VMEM((n_row, n_row, share, width), bf16),
            pltpu.VMEM((n_row, share, width), f32),
            pltpu.VMEM((n_row, width, share), bf16),
            pltpu.VMEM((width, block_cols), f32),
            pltpu.VMEM((cols_out, width, share), bf16),
            pltpu.VMEM((cols_out, width, share), bf16),
            pltpu.VMEM((width, share), bf16),
            pltpu.VMEM((n_col, width, share), bf16),
            pltpu.VMEM((n_col, width, share), f32),
            pltpu.VMEM((n_col, 2, share), f32),
            pltpu.VMEM((width, share), f32),
            dma((n_row,)),
            dma((cols_out,)), dma((cols_out,)),
            dma((n_row,)), dma((n_row, n_row)),
            dma((n_row, n_row)), dma((n_row,)),
            dma((cols_out,)), dma((cols_out,)),
            dma((n_col,)), dma((n_col,)),
            dma((cols_out,)), dma((cols_out,)),
            dma((cols_out,)), dma((cols_out,)),
        ],
        compiler_params=pltpu.CompilerParams(
            collective_id=0, has_side_effects=True, vmem_limit_bytes=56 * 2**20
        ),
    )(forcing, diag_inverse, coupling, inverse_factor)


def solution(mesh):
    placed = (
        P("sec", ("row", "col"), None),
        P("sec", None, "col", "row"),
        P("sec", None, "col"),
        P("sec", None, ("row", "col")),
    )
    n_sec, n_row, n_col = (mesh.shape[axis] for axis in ("sec", "row", "col"))

    def body(forcing, inverse_factor, diag_inverse, coupling):
        share, width = forcing.shape[1:]
        fits = inverse_factor.size * 2 <= 32 * 2**20
        if share % 128 or width % 128 or not fits or n_sec < 3:
            return local(forcing, inverse_factor, diag_inverse, coupling)
        return sweep(n_sec, n_row, n_col, forcing, inverse_factor, diag_inverse, coupling)

    return jax.shard_map(
        body, mesh=mesh, in_specs=placed, out_specs=P("sec", ("row", "col"), None), check_vma=False
    )
```

```python
import functools

import jax
import jax.numpy as jnp
from jax import lax
from jax.experimental import pallas as pl
from jax.experimental.pallas import tpu as pltpu
from jax.sharding import PartitionSpec as P


def shifted(value, axis, steps):
    count = lax.axis_size(axis)
    initial, last = (max(0, -steps), min(count, count - steps))
    return lax.ppermute(value, axis, [(source, source + steps) for source in range(initial, last)])


def complex_rows(coef_re, coef_im, values, half):
    v_re = values[:, :half]
    v_im = values[:, half:]
    out_re = coef_re[:, None] * v_re - coef_im[:, None] * v_im
    out_im = coef_re[:, None] * v_im + coef_im[:, None] * v_re
    return jnp.concatenate([out_re, out_im], axis=1)


def combine_stack(product):
    half = product.shape[2] // 2
    out_re = product[0, :, :half] - product[1, :, half:]
    out_im = product[0, :, half:] + product[1, :, :half]
    return jnp.concatenate([out_re, out_im], axis=1)


def solve_section(source, factor, dinv):
    width = source.shape[1]
    product = jnp.einsum(
        "kij,jb->kib",
        factor,
        lax.all_gather(source, "col", axis=0, tiled=True),
        preferred_element_type=jnp.float32,
    )
    forward = combine_stack(product)
    share = lax.psum_scatter(
        forward.astype(jnp.bfloat16), "row", scatter_dimension=0, tiled=True
    ).astype(jnp.float32)
    share_rows = share.shape[0]
    local_dinv = lax.dynamic_slice_in_dim(dinv, lax.axis_index("row") * share_rows, share_rows, 1)
    scaled = complex_rows(local_dinv[0], local_dinv[1], share, width // 2).astype(jnp.bfloat16)
    product = jnp.einsum(
        "kij,ib->kjb",
        factor,
        lax.all_gather(scaled, "row", axis=0, tiled=True),
        preferred_element_type=jnp.float32,
    )
    back = combine_stack(product)
    return lax.psum_scatter(
        back.astype(jnp.bfloat16), "col", scatter_dimension=0, tiled=True
    ).astype(jnp.float32)


def local(forcing, inverse_factor, diag_inverse, coupling):
    sections = lax.axis_size("sec")
    section_id = lax.axis_index("sec")
    local_rhs = forcing[0]
    factor = inverse_factor[0]
    dinv = diag_inverse[0]
    couple = coupling[0]
    rows_here = local_rhs.shape[0]
    half = local_rhs.shape[1] // 2
    block_count = 1
    block_width = half // block_count
    rhs_blocks = local_rhs.reshape(rows_here, 2, block_count, block_width)
    results = jnp.zeros((rows_here, 2, block_count, block_width), jnp.float32)
    outgoing = jnp.zeros((rows_here, 2 * block_width), jnp.float32)
    for step_index in range(block_count + sections - 1):
        if step_index > 0:
            incoming = shifted(outgoing.astype(jnp.bfloat16), "sec", 1).astype(outgoing.dtype)
        else:
            incoming = jnp.zeros((rows_here, 2 * block_width), jnp.float32)
        block_index = step_index - section_id
        active = jnp.logical_and(block_index >= 0, block_index < block_count)
        safe_index = jnp.clip(block_index, 0, block_count - 1)
        current = lax.dynamic_index_in_dim(rhs_blocks, safe_index, 2, keepdims=False)
        current = current.reshape(rows_here, 2 * block_width)
        source = (current - complex_rows(couple[0], couple[1], incoming, block_width)).astype(
            jnp.bfloat16
        )
        field = solve_section(source, factor, dinv)
        updated = lax.dynamic_update_index_in_dim(
            results, field.reshape(rows_here, 2, block_width), safe_index, 2
        )
        results = jnp.where(active, updated, results)
        outgoing = field
    return results.reshape(1, rows_here, 2 * half)


MESH = pl.DeviceIdType.MESH


def sweep_kernel(
    n_sec, n_row, n_col, forcing, dinv, coupling, factor_hbm, out,
    factor, src_a, src_b, part_out, part_in, own, scaled, back,
    cross_out, cross_in, prev_out, prev_in, forcing_t,
    coupling_all, result,
    load_sem, src_send, src_recv, part_send, part_recv,
    sc_send, sc_recv, cross_send, cross_recv, prev_send, prev_recv,
    rhs_send, rhs_recv, coef_send, coef_recv,
):
    share = own.shape[1]
    half = own.shape[2] // 2
    block_rows = n_row * share
    block_cols = n_col * share
    s, r, c = lax.axis_index("sec"), lax.axis_index("row"), lax.axis_index("col")

    def last_row(piece, col):
        return jnp.minimum(n_row - 1, (col * block_rows + (piece + 1) * share - 1) // block_cols)

    def piece_rows(piece):
        return pl.ds(pl.multiple_of(piece * share, share), share)

    def load(q):
        rows = piece_rows(q)
        return pltpu.make_async_copy(
            factor_hbm.at[0, :, rows, :], factor.at[:, rows, :], load_sem.at[q]
        )

    last = [last_row(q, c) for q in range(n_row)]
    owner = [(m + 1) // 2 for m in last]

    def send_source(j):
        return pltpu.make_async_remote_copy(
            src_ref=src_a.at[piece_rows(c)], dst_ref=src_a.at[piece_rows(c)],
            send_sem=src_send.at[j - 1], recv_sem=src_recv.at[j - 1],
            device_id=(s, r, lax.rem(c + j, n_col)), device_id_type=MESH,
        )

    inner = [
        jnp.logical_and(r != o, jnp.logical_and(r > 0, jnp.logical_or(r < o, r < m)))
        for o, m in zip(owner, last)
    ]

    def send_part(q, side):
        return pltpu.make_async_remote_copy(
            src_ref=part_out.at[q], dst_ref=part_in.at[q, side],
            send_sem=part_send.at[q], recv_sem=part_recv.at[q, side],
            device_id=(s, lax.rem(r + (1 if side == 0 else n_row - 1), n_row), c), device_id_type=MESH,
        )

    def start_part(q):
        for side in (0, 1):
            @pl.when((r < owner[q]) if side == 0 else (r > owner[q]))
            def _(side=side):
                send_part(q, side).start()

    def send_scaled(q, side):
        return pltpu.make_async_remote_copy(
            src_ref=scaled.at[q], dst_ref=scaled.at[q],
            send_sem=sc_send.at[q, side], recv_sem=sc_recv.at[q],
            device_id=(s, lax.rem(r + (1 if side == 0 else n_row - 1), n_row), c), device_id_type=MESH,
        )

    def passes_on(q, side):
        if side == 0:
            return jnp.logical_and(r >= owner[q], r < last[q])
        return jnp.logical_and(r <= owner[q], r > 0)

    def send_rhs(j):
        return pltpu.make_async_remote_copy(
            src_ref=forcing_t.at[c], dst_ref=forcing_t.at[c],
            send_sem=rhs_send.at[j - 1], recv_sem=rhs_recv.at[j - 1],
            device_id=(s, r, lax.rem(c + j, n_col)), device_id_type=MESH,
        )

    def send_coef(j):
        return pltpu.make_async_remote_copy(
            src_ref=coupling_all.at[c], dst_ref=coupling_all.at[c],
            send_sem=coef_send.at[j - 1], recv_sem=coef_recv.at[j - 1],
            device_id=(s, r, lax.rem(c + j, n_col)), device_id_type=MESH,
        )

    def send_cross(j):
        return pltpu.make_async_remote_copy(
            src_ref=cross_out.at[j - 1], dst_ref=cross_in.at[j - 1],
            send_sem=cross_send.at[j - 1], recv_sem=cross_recv.at[j - 1],
            device_id=(s, r, lax.rem(c + j, n_col)), device_id_type=MESH,
        )

    def send_prev(j):
        return pltpu.make_async_remote_copy(
            src_ref=prev_out, dst_ref=prev_in.at[j],
            send_sem=prev_send.at[j], recv_sem=prev_recv.at[j],
            device_id=(lax.rem(s + 1, n_sec), r, lax.rem(c + j, n_col)), device_id_type=MESH,
        )

    order = list(range(n_row - 1, -1, -1))
    for q in order:
        @pl.when(r <= last[q])
        def _(q=q):
            load(q).start()

    barrier = pltpu.get_barrier_semaphore()
    for i in range(1, n_row):
        pl.semaphore_signal(barrier, 1, device_id=(s, lax.rem(r + i, n_row), c), device_id_type=MESH)
    for j in range(1, n_col):
        pl.semaphore_signal(barrier, 1, device_id=(s, r, lax.rem(c + j, n_col)), device_id_type=MESH)
    for step in (1, n_sec - 1):
        for j in range(n_col):
            pl.semaphore_signal(
                barrier, 1, device_id=(lax.rem(s + step, n_sec), r, lax.rem(c + j, n_col)),
                device_id_type=MESH,
            )
    pl.semaphore_wait(barrier, n_row - 1 + n_col - 1 + 2 * n_col)

    def turned(value):
        return jnp.concatenate([-value[:, half:], value[:, :half]], axis=1)

    @pl.when(s == 0)
    def _():
        src_a[piece_rows(c), :] = forcing[0].astype(jnp.bfloat16)
        for j in range(1, n_col):
            send_source(j).start()
        for j in range(n_col):
            if j > 0:
                send_source(j).wait_recv()
            rows = piece_rows(lax.rem(c - j + n_col, n_col))
            src_b[rows, :] = turned(src_a[rows, :].astype(jnp.float32)).astype(jnp.bfloat16)

    @pl.when(s > 0)
    def _():
        forcing_t[c] = forcing[0].T
        coupling_all[c] = coupling[0]
        for j in range(1, n_col):
            send_rhs(j).start()
            send_coef(j).start()
        for j in range(1, n_col):
            send_rhs(j).wait_recv()
            send_coef(j).wait_recv()
        for j in range(n_col):
            col = lax.rem(c - j + n_col, n_col)
            rows = piece_rows(col)
            send_prev(j).wait_recv()
            previous = prev_in[j].astype(jnp.float32)
            p_re, p_im = previous[:half], previous[half:]
            c_re, c_im = coupling_all[col, 0:1, :], coupling_all[col, 1:2, :]
            new_re = forcing_t[col, :half] - (c_re * p_re - c_im * p_im)
            new_im = forcing_t[col, half:] - (c_re * p_im + c_im * p_re)
            src_a[rows, :] = jnp.concatenate([new_re, new_im], axis=0).T.astype(jnp.bfloat16)
            src_b[rows, :] = jnp.concatenate([-new_im, new_re], axis=0).T.astype(jnp.bfloat16)

    tile = min(512, share)

    def forward_piece(q):
        @pl.when(r <= last[q])
        def _():
            load(q).wait()
            @pl.loop(0, share // tile)
            def _(t):
                rows = pl.ds(pl.multiple_of(q * share + t * tile, tile), tile)
                here = pl.ds(pl.multiple_of(t * tile, tile), tile)
                total = jnp.dot(factor[0, rows, :], src_a[...], preferred_element_type=jnp.float32)
                total += jnp.dot(factor[1, rows, :], src_b[...], preferred_element_type=jnp.float32)
                own[q, here, :] = total
                part_out[q, here, :] = total.astype(jnp.bfloat16)

            @pl.when(jnp.logical_and(r != owner[q], jnp.logical_not(inner[q])))
            def _():
                start_part(q)

    def relay_part(q):
        for side in (0, 1):
            between = jnp.logical_and(r > 0, r < owner[q])
            if side == 1:
                between = jnp.logical_and(r > owner[q], r < last[q])

            @pl.when(between)
            def _(side=side):
                send_part(q, side).wait_recv()
                part_out[q] = (own[q] + part_in[q, side].astype(jnp.float32)).astype(jnp.bfloat16)
                send_part(q, side).start()

    def relay_scaled(q):
        for side in (0, 1):
            @pl.when(jnp.logical_and(passes_on(q, side), r != owner[q]))
            def _(side=side):
                send_scaled(q, side).wait_recv()
                send_scaled(q, side).start()

    def reduce_piece(q):
        @pl.when(r == owner[q])
        def _():
            for side in (0, 1):
                @pl.when((r > 0) if side == 0 else (r < last[q]))
                def _(side=side):
                    send_part(q, side).wait_recv()
                    own[q] += part_in[q, side].astype(jnp.float32)

            forward = own[q].T
            d_re, d_im = dinv[0, 0:1, pl.ds(q * share, share)], dinv[0, 1:2, pl.ds(q * share, share)]
            f_re, f_im = forward[:half], forward[half:]
            scaled[q] = jnp.concatenate(
                [d_re * f_re - d_im * f_im, d_re * f_im + d_im * f_re], axis=0
            ).astype(jnp.bfloat16)
            for side in (0, 1):
                @pl.when(passes_on(q, side))
                def _(side=side):
                    send_scaled(q, side).start()

    for i, q in enumerate(order):
        forward_piece(q)
        if i >= 1:
            relay_part(order[i - 1])
    relay_part(order[-1])
    for q in order:
        reduce_piece(q)

    back[...] = jnp.zeros_like(back)
    width = min(512, share)
    filled = r <= last[n_row - 1]
    turns = list(range(1, n_row, 2)) + list(range(0, n_row, 2))
    relayed = []
    for i, q in enumerate(turns):
        for piece in (order[i], q):
            if piece not in relayed:
                relayed.append(piece)
                relay_scaled(piece)
        ends = jnp.logical_or(r == last[q], r == 0)

        @pl.when(jnp.logical_and(jnp.logical_and(r <= last[q], r != owner[q]), ends))
        def _(q=q):
            send_scaled(q, 0).wait_recv()

        for j in list(range(1, n_col)) + [0]:
            @pl.when(r <= last[q])
            def _(q=q, j=j):
                rows = piece_rows(q)
                lhs = scaled[q]
                lhs_b = jnp.concatenate([-lhs[half:], lhs[:half]], axis=0)

                @pl.loop(0, share // width)
                def _(t):
                    first = lax.rem(c + j, n_col) * share + t * width
                    cols = pl.ds(pl.multiple_of(first, width), width)
                    total = jnp.dot(lhs, factor[0, rows, cols], preferred_element_type=jnp.float32)
                    total += jnp.dot(lhs_b, factor[1, rows, cols], preferred_element_type=jnp.float32)
                    back[:, cols] += total

            if q == turns[-1] and j > 0:
                @pl.when(filled)
                def _(j=j):
                    cross_out[j - 1] = back[:, piece_rows(lax.rem(c + j, n_col))].astype(jnp.bfloat16)
                    send_cross(j).start()

    result[...] = back[:, piece_rows(c)]
    for j in range(1, n_col):
        @pl.when(r <= last_row(n_row - 1, lax.rem(c - j + n_col, n_col)))
        def _(j=j):
            send_cross(j).wait_recv()
            result[...] += cross_in[j - 1].astype(jnp.float32)

    @pl.when(s < n_sec - 1)
    def _():
        prev_out[...] = result[...].astype(jnp.bfloat16)
        for j in list(range(1, n_col)) + [0]:
            send_prev(j).start()

    out[0] = result[...].T

    @pl.when(s == 0)
    def _():
        for j in range(1, n_col):
            send_source(j).wait_send()

    @pl.when(s > 0)
    def _():
        for j in range(1, n_col):
            send_rhs(j).wait_send()
            send_coef(j).wait_send()

    @pl.when(filled)
    def _():
        for j in range(1, n_col):
            send_cross(j).wait_send()

    for q in range(n_row):
        @pl.when(jnp.logical_and(r <= last[q], r != owner[q]))
        def _(q=q):
            send_part(q, 0).wait_send()

        for side in (0, 1):
            @pl.when(passes_on(q, side))
            def _(q=q, side=side):
                send_scaled(q, side).wait_send()

    @pl.when(s < n_sec - 1)
    def _():
        for j in range(n_col):
            send_prev(j).wait_send()


def sweep(n_sec, n_row, n_col, forcing, inverse_factor, diag_inverse, coupling):
    share, width = forcing.shape[1:]
    block_rows, block_cols = inverse_factor.shape[2:]
    vmem = pl.BlockSpec(memory_space=pltpu.VMEM)
    bf16, f32 = jnp.bfloat16, jnp.float32
    dma = pltpu.SemaphoreType.DMA
    cols_out = max(n_col - 1, 1)
    return pl.pallas_call(
        functools.partial(sweep_kernel, n_sec, n_row, n_col),
        out_shape=jax.ShapeDtypeStruct(forcing.shape, f32),
        in_specs=[vmem, vmem, vmem, pl.BlockSpec(memory_space=pl.ANY)],
        out_specs=vmem,
        scratch_shapes=[
            pltpu.VMEM((2, block_rows, block_cols), bf16),
            pltpu.VMEM((block_cols, width), bf16),
            pltpu.VMEM((block_cols, width), bf16),
            pltpu.VMEM((n_row, share, width), bf16),
            pltpu.VMEM((n_row, 2, share, width), bf16),
            pltpu.VMEM((n_row, share, width), f32),
            pltpu.VMEM((n_row, width, share), bf16),
            pltpu.VMEM((width, block_cols), f32),
            pltpu.VMEM((cols_out, width, share), bf16),
            pltpu.VMEM((cols_out, width, share), bf16),
            pltpu.VMEM((width, share), bf16),
            pltpu.VMEM((n_col, width, share), bf16),
            pltpu.VMEM((n_col, width, share), f32),
            pltpu.VMEM((n_col, 2, share), f32),
            pltpu.VMEM((width, share), f32),
            dma((n_row,)),
            dma((cols_out,)), dma((cols_out,)),
            dma((n_row,)), dma((n_row, 2)),
            dma((n_row, 2)), dma((n_row,)),
            dma((cols_out,)), dma((cols_out,)),
            dma((n_col,)), dma((n_col,)),
            dma((cols_out,)), dma((cols_out,)),
            dma((cols_out,)), dma((cols_out,)),
        ],
        compiler_params=pltpu.CompilerParams(
            collective_id=0, has_side_effects=True, vmem_limit_bytes=56 * 2**20
        ),
    )(forcing, diag_inverse, coupling, inverse_factor)


def solution(mesh):
    placed = (
        P("sec", ("row", "col"), None),
        P("sec", None, "col", "row"),
        P("sec", None, "col"),
        P("sec", None, ("row", "col")),
    )
    n_sec, n_row, n_col = (mesh.shape[axis] for axis in ("sec", "row", "col"))

    def body(forcing, inverse_factor, diag_inverse, coupling):
        share, width = forcing.shape[1:]
        fits = inverse_factor.size * 2 <= 32 * 2**20
        if share % 128 or width % 128 or not fits or n_sec < 3:
            return local(forcing, inverse_factor, diag_inverse, coupling)
        return sweep(n_sec, n_row, n_col, forcing, inverse_factor, diag_inverse, coupling)

    return jax.shard_map(
        body, mesh=mesh, in_specs=placed, out_specs=P("sec", ("row", "col"), None), check_vma=False
    )
```
